768 devices in a mesh: nodes: 128 (over x, y, z_hi), years: 6 (over z_lo, core).
Axes of the slice: x: 4, y: 8, z: 12 (z_hi: 4, z_lo: 3; z = z_hi * 3 + z_lo), core: 2. Of those that a mesh axis runs over, the one named last changes fastest.
Arguments:
- features: float32 [65536, 768], P('nodes', 'years'), may hold values from -6 to 6
- weight: float32 [768, 512], P('years'), may hold values from -0.21875 to 0.21875
- bias: float32 [512], replicated, may hold values from -3 to 3
- tile_weights: float32 [512, 4, 128, 128], P('nodes'), may hold values from 0.0001 to 0.5, as said below
- tile_offsets: int32 [512, 4], P('nodes'), may hold values from -8 to 8, as said below
- tile_counts: int32 [512], P('nodes'), may hold values from 1 to 4
- grad_out: float32 [65536, 512], P('nodes'), may hold values from -6 to 6
Outputs:
- output: float32 [65536, 512], P('nodes')
- grad_features: float32 [65536, 768], P('nodes', 'years')
- grad_weight: float32 [768, 512], P('years')
- grad_bias: float32 [512], replicated
The draws below stay inside these ranges and needn't reach their ends.
Inputs may be any that keep to these rules, and one draw needn't show every extreme that they name: `tile_weights`: Positive. `tile_offsets`: the live slots of a row tile name distinct offsets; slots at or past tile_counts are ignored.
All inputs are finite; a program needn't handle non-finite values.
Results may differ from the reference program's by a relative error of at most 0.0001.
Values sent between devices are 32-bit elements; how exact they have to be, the bound alone decides.
No kernel may reach another device: no remote copies, remote signals or barrier semaphores. Data moves between devices by JAX's collectives and lax.ppermute only.
A program may use at most 64 MiB of HBM per device.

```python
import math
import jax
import jax.numpy as jnp
from jax import lax

TILE = 128
TPD = 4
SLOTS = 4
REACH = 2
H = 512
F = 768
NTILES = 512
NODES = 65536


def log_draw(key, shape, low, high):
    return jnp.exp(jax.random.uniform(key, shape, jnp.float32, math.log(low), math.log(high)))


def draw_tile_weights(key, part):
    key_base, key_row, key_col = jax.random.split(key, 3)
    shape = (NTILES, SLOTS, TILE, TILE)
    base = log_draw(key_base, shape, 0.004, 0.04)
    row_scale = log_draw(key_row, (NTILES, 1, TILE, 1), 0.3, 3.0)
    col_scale = log_draw(key_col, (NTILES, SLOTS, 1, TILE), 0.3, 3.0)
    return base * row_scale * col_scale


def one_order(key_one):
    return jax.random.permutation(key_one, 2 * REACH * TPD + 1)


def draw_tile_offsets(key, part):
    band = REACH * TPD
    span = 2 * band + 1
    keys = jax.random.split(key, NTILES)
    orders = jax.vmap(one_order)(keys).astype(jnp.int32)
    row_ids = jnp.arange(NTILES, dtype=jnp.int32)
    target = jnp.where(row_ids == 0, 2 * band, jnp.where(row_ids == 1, 0, -1)).astype(jnp.int32)
    first = jnp.argmax(orders == target[:, None], axis=1).astype(jnp.int32)
    place = (jnp.arange(span, dtype=jnp.int32)[None, :] + first[:, None]) % span
    rolled = jnp.take_along_axis(orders, place, axis=1)
    return (rolled[:, :SLOTS] - band).astype(jnp.int32)


def draw_tile_counts(key, part):
    counts = jax.random.randint(key, (NTILES,), 1, SLOTS + 1).astype(jnp.int32)
    return counts.at[:2].set(SLOTS)


def level_of(stream_key, shape, cuts, smallest, largest):
    factor_of = 1.0
    for axis_at, shards_of in cuts:
        steps = jax.random.uniform(jax.random.fold_in(jax.random.fold_in(stream_key, 6), axis_at), (shards_of,), jnp.float32, smallest / len(cuts), largest / len(cuts))
        factor_of = factor_of * jnp.repeat(jnp.exp(steps), shape[axis_at] // shards_of).reshape((-1,) + (1,) * (len(shape) - 1 - axis_at))
    return factor_of


def scatter_about(rng, extent, width, bound, shards=(), held_as=jnp.bfloat16):
    values = jax.random.normal(rng, extent, jnp.float32) * width
    if len(shards) > 0:
        values = level_of(rng, extent, shards, -0.22, 0.18) * values
    return jnp.clip(values, min=-bound, max=bound).astype(held_as)


def setup_inputs(seed: int = 0) -> dict:
    arg_keys = jax.random.split(jax.random.key(seed), 8)
    return {
        "features": scatter_about(arg_keys[0], (NODES, F), 1.0, 6.0, ((0, 128), (1, 6)), jnp.float32),
        "weight": scatter_about(arg_keys[1], (F, H), F ** -0.5, 0.21875, ((0, 6),), jnp.float32),
        "bias": scatter_about(arg_keys[2], (H,), 0.5, 3.0, (), jnp.float32),
        "tile_weights": draw_tile_weights(jax.random.fold_in(arg_keys[7], 71), 0),
        "tile_offsets": draw_tile_offsets(jax.random.fold_in(arg_keys[7], 71), 0),
        "tile_counts": draw_tile_counts(jax.random.fold_in(arg_keys[7], 71), 0),
        "grad_out": scatter_about(arg_keys[6], (NODES, H), 1.0, 6.0, ((0, 128),), jnp.float32),
    }


def reference(features, weight, bias, tile_weights, tile_offsets, tile_counts, grad_out):
    highest = lax.Precision.HIGHEST
    row_tiles = tile_weights.shape[0]
    slot_total = tile_weights.shape[1]
    tile_size = tile_weights.shape[2]
    feat_width = features.shape[1]
    live = (jnp.arange(slot_total, dtype=jnp.int32)[None, :] < tile_counts[:, None]).astype(jnp.float32)
    masked = tile_weights * live[:, :, None, None]
    degree = 1.0 + jnp.sum(masked, axis=(1, 3))
    columns = (jnp.arange(row_tiles, dtype=jnp.int32)[:, None] + tile_offsets) % row_tiles
    tiled = features.reshape(row_tiles, tile_size, feat_width)
    gathered_sum = jnp.zeros_like(tiled)
    for slot in range(slot_total):
        gathered_sum = gathered_sum + jnp.einsum("tij,tjf->tif", masked[:, slot], tiled[columns[:, slot]], precision=highest)
    mixed = ((gathered_sum + tiled) / degree[:, :, None]).reshape(-1, feat_width)
    pre = jnp.dot(mixed, weight, precision=highest, preferred_element_type=jnp.float32) + bias
    sigma = jax.nn.sigmoid(pre)
    output = pre * sigma
    grad_pre = grad_out * sigma * (1.0 + pre * (1.0 - sigma))
    grad_weight = jnp.dot(mixed.T, grad_pre, precision=highest, preferred_element_type=jnp.float32)
    grad_bias = jnp.sum(grad_pre, axis=0)
    scaled = grad_pre.reshape(row_tiles, tile_size, -1) / degree[:, :, None]
    back_sum = scaled
    for slot in range(slot_total):
        contrib = jnp.einsum("tij,tif->tjf", masked[:, slot], scaled, precision=highest)
        back_sum = back_sum.at[columns[:, slot]].add(contrib)
    grad_features = jnp.dot(back_sum.reshape(-1, back_sum.shape[2]), weight.T, precision=highest, preferred_element_type=jnp.float32)
    return output, grad_features, grad_weight, grad_bias
```

```python
import jax
import jax.numpy as jnp
from jax import lax
from jax.experimental import pallas as pl
from jax.experimental.pallas import tpu as pltpu
from jax.sharding import Mesh, PartitionSpec as P

NODES = ("x", "y", "zh")
YEARS = ("zl", "c")
PLANE = ("x", "y")
REACH = 2
T = 128
F32 = jnp.float32
BF = jnp.bfloat16
VMEM = pl.BlockSpec(memory_space=pltpu.VMEM)
SMEM = pl.BlockSpec(memory_space=pltpu.SMEM)


def shape_of(shape, dtype=F32):
    return jax.ShapeDtypeStruct(shape, dtype)


def call(kernel, ins, outs, scratch, flops, bytes_accessed, name):
    return pl.pallas_call(
        kernel,
        in_specs=ins,
        out_specs=[VMEM] * len(outs),
        out_shape=outs,
        scratch_shapes=scratch,
        name=name,
        cost_estimate=pl.CostEstimate(
            flops=flops, bytes_accessed=bytes_accessed, transcendentals=0
        ),
        compiler_params=pltpu.CompilerParams(vmem_limit_bytes=40 * 1024 * 1024),
    )


def split(v):
    hi = v.astype(BF)
    lo = (v - hi.astype(F32)).astype(BF)
    return hi, lo


def dot(a, b):
    return lax.dot_general(a, b, (((1,), (0,)), ((), ())), preferred_element_type=F32)


def prepare_kernel(count, tiles, weight, a_hi, a_lo, t_hi, t_lo, rdeg, wt):
    for t in range(tiles.shape[0]):
        total = jnp.zeros((T, T), F32)
        for s in range(tiles.shape[1]):
            live = jnp.where(s < count[t], 1.0, 0.0).astype(F32)
            a = tiles[t, s] * live
            total = total + a
            cols = slice(s * T, (s + 1) * T)
            hi, lo = split(a)
            a_hi[t, :, cols] = hi
            a_lo[t, :, cols] = lo
            hi, lo = split(a.T)
            t_hi[t, cols, :] = hi
            t_lo[t, cols, :] = lo
        degree = 1.0 + jnp.sum(total, axis=1, keepdims=True)
        rdeg[t * T : (t + 1) * T, :] = jnp.broadcast_to(1.0 / degree, (T, T))
    for k in range(weight.shape[1] // T):
        hi, lo = split(weight[:, k * T : (k + 1) * T].T)
        wt[k * T : (k + 1) * T, :T] = hi
        wt[k * T : (k + 1) * T, T:] = lo


def mix_kernel(index, m2, m1, own, p1, p2, a_hi, a_lo, rdeg, mixed, window):
    rows = own.shape[0]
    for q, ref in enumerate((m2, m1, own, p1, p2)):
        hi, lo = split(ref[...])
        window[q * rows : (q + 1) * rows, :T] = hi
        window[q * rows : (q + 1) * rows, T:] = lo
    for t in range(a_hi.shape[0]):
        picked = []
        for s in range(4):
            at = pl.multiple_of(index[t * 4 + s] * T, T)
            picked.append(window[pl.ds(at, T), :])
        b = jnp.concatenate(picked, axis=0)
        wide = dot(a_hi[t], b)
        total = wide[:, :T] + wide[:, T:] + dot(a_lo[t], b[:, :T])
        r = slice(t * T, (t + 1) * T)
        mixed[r, :] = (total + own[r, :]) * rdeg[r, :]


def layer_kernel(
    index, slot, x0, x1, x2, y, w0, w1, w2, v, bias, gout, rdeg, t_hi, t_lo, wt,
    output, gpre, q0, q1, q2, q3, q4, m_hi, m_lo, w_hi, w_lo, back,
):
    rows = gout.shape[0]
    for k in range(6):
        m = (x0, x1, x2)[k][...] if k < 3 else y[(k - 3) * rows : (k - 2) * rows, :]
        w = (w0, w1, w2)[k][...] if k < 3 else v[(k - 3) * T : (k - 2) * T, :]
        hi, lo = split(m)
        m_hi[slot[k]] = hi
        m_lo[slot[k]] = lo
        hi, lo = split(w)
        w_hi[pl.ds(pl.multiple_of(slot[k] * T, T), T), :] = hi
        w_lo[pl.ds(pl.multiple_of(slot[k] * T, T), T), :] = lo
    back[...] = jnp.zeros_like(back)
    wth = wt[:, :T]
    for t in range(rows // T):
        r = slice(t * T, (t + 1) * T)
        mh = jnp.concatenate([m_hi[k, r, :] for k in range(6)], axis=1)
        ml = jnp.concatenate([m_lo[k, r, :] for k in range(6)], axis=1)
        pre = dot(mh, w_hi[...]) + dot(mh, w_lo[...]) + dot(ml, w_hi[...]) + bias[...]
        sigma = 1.0 / (1.0 + jnp.exp(-pre))
        output[r, :] = pre * sigma
        g = gout[r, :] * sigma * (1.0 + pre * (1.0 - sigma))
        gpre[r, :] = g
        scale = rdeg[r, :]
        scaled = g * jnp.concatenate([scale] * 4, axis=1)
        sh, sl = split(scaled)
        wide = dot(sh, wt[...])
        z = wide[:, :T] + wide[:, T:] + dot(sl, wth)
        zh, zl = split(z)
        wide = dot(t_hi[t], jnp.concatenate([zh, zl], axis=1))
        contrib = wide[:, :T] + wide[:, T:] + dot(t_lo[t], zh)
        back[REACH * rows + t * T : REACH * rows + (t + 1) * T, :] += z
        for s in range(4):
            at = pl.multiple_of(index[t * 4 + s] * T, T)
            back[pl.ds(at, T), :] += contrib[s * T : (s + 1) * T, :]
    for q, ref in enumerate((q0, q1, q2, q3, q4)):
        ref[...] = back[q * rows : (q + 1) * rows, :]


def weight_kernel(mixed, gpre, pieces):
    rows = mixed.shape[0]
    m = jnp.concatenate([mixed[t * T : (t + 1) * T, :].T for t in range(rows // T)], axis=1)
    mh, ml = split(m)
    for k in range(4):
        g = gpre[:, k * T : (k + 1) * T]
        gh, gl = split(g)
        wide = dot(mh, jnp.concatenate([gh, gl], axis=1))
        total = wide[:, :T] + wide[:, T:] + dot(ml, gh)
        for b in range(8):
            pieces[b * 4 + k, 0:16, :] = total[b * 16 : (b + 1) * 16, :]
        line = jnp.sum(g, axis=0, keepdims=True)
        for p in range(32):
            pieces[p, 16 + k : 17 + k, :] = line
    for p in range(32):
        pieces[p, 20:24, :] = jnp.zeros((4, T), F32)


def passed_along(block, axis, distance):
    devices = range(lax.axis_size(axis))
    route = [((i - distance) % len(devices), i) for i in devices]
    return lax.ppermute(block, axis, route)


def body(features, weight, bias, tile_weights, tile_offsets, tile_counts, grad_out):
    rows, width = features.shape
    tiles = tile_weights.shape[0]
    index = jnp.arange(tiles, dtype=jnp.int32)[:, None] + tile_offsets + REACH * tiles
    index = jnp.clip(index, 0, (2 * REACH + 1) * tiles - 1).reshape(-1)
    zl = lax.axis_index("zl")
    c = lax.axis_index("c")
    place = [((zl - d) % 3) * 2 + c for d in range(3)]
    place += [((zl - d) % 3) * 2 + 1 - c for d in range(3)]
    slot = jnp.stack(place).astype(jnp.int32)

    with jax.named_scope("halo"):
        from_below = passed_along(features, NODES, 1)
        from_above = passed_along(features, NODES, -1)
        from_below2 = passed_along(from_below, NODES, 1)
        from_above2 = passed_along(from_above, NODES, -1)
    with jax.named_scope("weight_gather"):
        w1 = passed_along(weight, "zl", 1)
        w2 = passed_along(weight, "zl", 2)
        v = passed_along(jnp.concatenate([weight, w1, w2], axis=0), "c", 1)

    a_hi, a_lo, t_hi, t_lo, rdeg, wt = call(
        prepare_kernel,
        [SMEM, VMEM, VMEM],
        [
            shape_of((tiles, T, 4 * T), BF),
            shape_of((tiles, T, 4 * T), BF),
            shape_of((tiles, 4 * T, T), BF),
            shape_of((tiles, 4 * T, T), BF),
            shape_of((rows, T)),
            shape_of((4 * T, 2 * T), BF),
        ],
        [],
        10**6,
        4 * 10**6,
        "prepare",
    )(tile_counts, tile_weights, weight)
    (mixed,) = call(
        mix_kernel,
        [SMEM] + [VMEM] * 8,
        [shape_of((rows, width))],
        [pltpu.VMEM((5 * rows, 2 * T), BF)],
        2 * 10**8,
        3 * 10**6,
        "mix",
    )(index, from_below2, from_below, features, from_above, from_above2, a_hi, a_lo, rdeg)
    with jax.named_scope("mixed_gather"):
        x1 = passed_along(mixed, "zl", 1)
        x2 = passed_along(mixed, "zl", 2)
        y = passed_along(jnp.concatenate([mixed, x1, x2], axis=0), "c", 1)
    piece = shape_of((rows, width))
    output, gpre, q0, q1, q2, q3, q4 = call(
        layer_kernel,
        [SMEM] * 2 + [VMEM] * 14,
        [shape_of((rows, 4 * T)), shape_of((rows, 4 * T))] + [piece] * 5,
        [
            pltpu.VMEM((6, rows, T), BF),
            pltpu.VMEM((6, rows, T), BF),
            pltpu.VMEM((6 * T, 4 * T), BF),
            pltpu.VMEM((6 * T, 4 * T), BF),
            pltpu.VMEM((5 * rows, T), F32),
        ],
        15 * 10**8,
        10**7,
        "layer",
    )(
        index, slot, mixed, x1, x2, y, weight, w1, w2, v, bias.reshape(1, -1), grad_out, rdeg,
        t_hi, t_lo, wt,
    )
    with jax.named_scope("back_halo"):
        up = passed_along(q4, NODES, 1)
        down = passed_along(q0, NODES, -1)
    (pieces,) = call(
        weight_kernel,
        [VMEM] * 2,
        [shape_of((32, 24, T))],
        [],
        2 * 10**8,
        2 * 10**6,
        "weight_grad",
    )(mixed, gpre)
    with jax.named_scope("nodes_sum"):
        held = jnp.sum(lax.all_to_all(pieces, PLANE, 0, 0), axis=0)
    with jax.named_scope("back_halo"):
        up = passed_along(q3 + up, NODES, 1)
        down = passed_along(q1 + down, NODES, -1)
    with jax.named_scope("nodes_sum"):
        held = jnp.broadcast_to(held[None], (4, 24, T))
        held = jnp.sum(lax.all_to_all(held, "zh", 0, 0), axis=0)
        grad_bias = held[16:20].reshape(-1)
        whole = jnp.broadcast_to(held[None, :16], (32, 16, T))
        whole = lax.all_to_all(whole, PLANE, 0, 0)
        grad_weight = whole.reshape(8, 4, 16, T).transpose(0, 2, 1, 3).reshape(T, 4 * T)
    grad_features = q2 + up + down
    return output, grad_features, grad_weight, grad_bias


def solution(mesh):
    fine = Mesh(mesh.devices.reshape(4, 8, 4, 3, 2), NODES + YEARS)
    placed = (
        P(NODES, YEARS),
        P(YEARS, None),
        P(),
        P(NODES, None, None, None),
        P(NODES, None),
        P(NODES),
        P(NODES, None),
    )
    return jax.shard_map(
        body,
        mesh=fine,
        in_specs=placed,
        out_specs=(P(NODES, None), P(NODES, YEARS), P(YEARS, None), P()),
        check_vma=False,
    )
```

```python
import jax
import jax.numpy as jnp
from jax import lax
from jax.experimental import pallas as pl
from jax.experimental.pallas import tpu as pltpu
from jax.sharding import Mesh, PartitionSpec as P

NODES = ("x", "y", "zh")
YEARS = ("zl", "c")
PLANE = ("x", "y")
REACH = 2
T = 128
F32 = jnp.float32
BF = jnp.bfloat16
VMEM = pl.BlockSpec(memory_space=pltpu.VMEM)
SMEM = pl.BlockSpec(memory_space=pltpu.SMEM)


def shape_of(shape, dtype=F32):
    return jax.ShapeDtypeStruct(shape, dtype)


def call(kernel, ins, outs, scratch, flops, bytes_accessed, name, limit):
    return pl.pallas_call(
        kernel,
        in_specs=ins,
        out_specs=[VMEM] * len(outs),
        out_shape=outs,
        scratch_shapes=scratch,
        name=name,
        cost_estimate=pl.CostEstimate(
            flops=flops, bytes_accessed=bytes_accessed, transcendentals=0
        ),
        compiler_params=pltpu.CompilerParams(vmem_limit_bytes=limit * 2**20),
    )


def split(v):
    hi = v.astype(BF)
    lo = (v - hi.astype(F32)).astype(BF)
    return hi, lo


def dot(a, b):
    return lax.dot_general(a, b, (((1,), (0,)), ((), ())), preferred_element_type=F32)


def dot_t(a, b):
    return lax.dot_general(a, b, (((1,), (1,)), ((), ())), preferred_element_type=F32)


def prepare_kernel(count, tiles, a_hi, a_lo, t_hl, rdeg):
    for t in range(tiles.shape[0]):
        total = jnp.zeros((T, T), F32)
        for s in range(tiles.shape[1]):
            live = jnp.where(s < count[t], 1.0, 0.0).astype(F32)
            a = tiles[t, s] * live
            total = total + a
            cols = slice(s * T, (s + 1) * T)
            hi, lo = split(a)
            a_hi[t, :, cols] = hi
            a_lo[t, :, cols] = lo
            hi, lo = split(a.T)
            t_hl[t, cols, :T] = hi
            t_hl[t, cols, T:] = lo
        degree = 1.0 + jnp.sum(total, axis=1, keepdims=True)
        rdeg[t * T : (t + 1) * T, :] = jnp.broadcast_to(1.0 / degree, (T, T))


def window_index(offset, t, s):
    return jnp.clip(t + offset[t, s] + 2 * 4, 0, 19)


def mix_kernel(where, offset, far, near, own, a_hi, a_lo, partial, window):
    rows = own.shape[1]
    c = where[0]
    for ref, shard in ((far, 4 * c), (near, 1 + 2 * c), (own, 2)):
        at = pl.multiple_of(shard * rows, rows)
        for k in range(2):
            hi, lo = split(ref[k])
            window[pl.ds(at, rows), k * T : (k + 1) * T] = hi
            window[pl.ds(at, rows), (2 + k) * T : (3 + k) * T] = lo
    window[5 * rows :, :] = jnp.zeros((T, 4 * T), BF)
    low, high = 12 * c, 12 + 8 * c
    first = (1 - c).astype(F32)
    for t in range(a_hi.shape[0]):
        picked = []
        for s in range(4):
            w = window_index(offset, t, s)
            w = jnp.where((w >= low) & (w < high), w, 20)
            picked.append(window[pl.ds(pl.multiple_of(w * T, T), T), :])
        b = jnp.concatenate(picked, axis=0)
        wide = dot(a_hi[t], b)
        total = wide[:, : 2 * T] + wide[:, 2 * T :] + dot(a_lo[t], b[:, : 2 * T])
        r = slice(t * T, (t + 1) * T)
        for k in range(2):
            partial[k, r, :] = total[:, k * T : (k + 1) * T] + own[k, r, :] * first


def layer_kernel(
    where, offset, mixed, got, swapped, weight, weight_got, weight_swapped, bias, gout, rdeg, t_hl,
    output, parts, far, near, center, m_hi, m_lo, w_hi, w_lo, s_hi, s_lo, g_hi, g_lo, back,
):
    rows = gout.shape[0]
    c, zl = where[0], where[1]
    arrived = ((mixed, weight, 0), (got, weight_got, 1 + c), (swapped, weight_swapped, 2 - c))
    for ref, ref_w, back_by in arrived:
        chip = lax.rem(zl - back_by + 3, 3)
        for k in range(2):
            hi, lo = split(ref[k])
            m_hi[chip * 2 + k] = hi
            m_lo[chip * 2 + k] = lo
            hi, lo = split(ref_w[k])
            at = pl.ds(pl.multiple_of((chip * 2 + k) * T, T), T)
            w_hi[at, :] = hi
            w_lo[at, :] = lo
    back[...] = jnp.zeros_like(back)
    line = jnp.zeros((1, 4 * T), F32)
    for t in range(rows // T):
        r = slice(t * T, (t + 1) * T)
        mh = jnp.concatenate([m_hi[k, r, :] for k in range(6)], axis=1)
        ml = jnp.concatenate([m_lo[k, r, :] for k in range(6)], axis=1)
        pre = dot(mh, w_hi[...]) + dot(mh, w_lo[...]) + dot(ml, w_hi[...]) + bias[...]
        sigma = 1.0 / (1.0 + jnp.exp(-pre))
        output[r, :] = pre * sigma
        g = gout[r, :] * sigma * (1.0 + pre * (1.0 - sigma))
        line = line + jnp.sum(g, axis=0, keepdims=True)
        hi, lo = split(g)
        g_hi[r, :] = hi
        g_lo[r, :] = lo
        scale = rdeg[r, :]
        hi, lo = split(g * jnp.concatenate([scale] * 4, axis=1))
        s_hi[r, :] = hi
        s_lo[r, :] = lo
    mine = pl.ds(pl.multiple_of(zl * (2 * T), 2 * T), 2 * T)
    wh, wl = w_hi[mine, :], w_lo[mine, :]
    z = dot_t(s_hi[...], wh) + dot_t(s_hi[...], wl) + dot_t(s_lo[...], wh)
    back[REACH * rows : (REACH + 1) * rows, :] = z
    zh, zo = split(z)
    for t in range(rows // T):
        r = slice(t * T, (t + 1) * T)
        both = jnp.concatenate([zh[r, :], zh[r, :]], axis=0)
        contrib = dot(t_hl[t], both) + dot(t_hl[t, :, :T], zo[r, :])
        for s in range(4):
            at = pl.multiple_of(window_index(offset, t, s) * T, T)
            back[pl.ds(at, T), :] += contrib[s * T : (s + 1) * T, :]
    far[...] = back[pl.ds(pl.multiple_of((4 - 4 * c) * rows, rows), rows), :]
    near[...] = back[pl.ds(pl.multiple_of((3 - 2 * c) * rows, rows), rows), :]
    mid = back[REACH * rows : (REACH + 1) * rows, :]
    center[...] = jnp.where(c == 0, mid[:, :T], mid[:, T:])
    own = mixed[c]
    m = jnp.concatenate([own[t * T : (t + 1) * T, :].T for t in range(rows // T)], axis=1)
    mh, ml = split(m)
    total = dot(mh, g_hi[...]) + dot(mh, g_lo[...]) + dot(ml, g_hi[...])
    for p in range(32):
        cols = slice((p % 4) * T, (p % 4 + 1) * T)
        parts[p, 0:16, :] = total[(p // 4) * 16 : (p // 4 + 1) * 16, cols]
        for k in range(4):
            parts[p, 16 + k : 17 + k, :] = line[:, k * T : (k + 1) * T]
        parts[p, 20:24, :] = jnp.zeros((4, T), F32)


def arrange_kernel(pieces, out):
    for p in range(32):
        out[(p // 4) * 16 : (p // 4 + 1) * 16, (p % 4) * T : (p % 4 + 1) * T] = pieces[p]


def by_core(block, axis, first, second):
    n = lax.axis_size(axis)
    route = [(2 * i + c, 2 * ((i + d) % n) + c) for i in range(n) for c, d in ((0, first), (1, second))]
    axes = (axis if isinstance(axis, tuple) else (axis,)) + ("c",)
    return lax.ppermute(block, axes, route)


def swap(block):
    return lax.ppermute(block, "c", [(0, 1), (1, 0)])


def body(features, weight, bias, tile_weights, tile_offsets, tile_counts, grad_out):
    rows, width = features.shape
    tiles = tile_weights.shape[0]
    zl, c = lax.axis_index("zl"), lax.axis_index("c")
    where = jnp.stack([c, zl]).astype(jnp.int32)

    with jax.named_scope("halo"):
        other = swap(features)
        pair = jnp.where(c == 0, jnp.stack([features, other]), jnp.stack([other, features]))
        near = by_core(pair, NODES, 1, -1)
        far = by_core(near, NODES, 1, -1)
    with jax.named_scope("weight_gather"):
        other_weight = swap(weight)
        mine = jnp.where(c == 0, jnp.stack([weight, other_weight]), jnp.stack([other_weight, weight]))
        mine, near = lax.optimization_barrier((mine, near))
        weight_got = by_core(mine, "zl", 1, 2)
        weight_swapped = swap(weight_got)

    a_hi, a_lo, t_hl, rdeg = call(
        prepare_kernel,
        [SMEM, VMEM],
        [
            shape_of((tiles, T, 4 * T), BF),
            shape_of((tiles, T, 4 * T), BF),
            shape_of((tiles, 4 * T, 2 * T), BF),
            shape_of((rows, T)),
        ],
        [],
        10**6,
        4 * 10**6,
        "prepare",
        8,
    )(tile_counts, tile_weights)
    (partial,) = call(
        mix_kernel,
        [SMEM] * 2 + [VMEM] * 5,
        [shape_of((2, rows, width))],
        [pltpu.VMEM((5 * rows + T, 4 * T), BF)],
        2 * 10**8,
        3 * 10**6,
        "mix",
        12,
    )(where, tile_offsets, far, near, pair, a_hi, a_lo)
    with jax.named_scope("mixed_gather"):
        mixed = (partial + swap(partial)) * rdeg[None]
        got = by_core(mixed, "zl", 1, 2)
        swapped = swap(got)
    output, parts, q_far, q_near, center = call(
        layer_kernel,
        [SMEM] * 2 + [VMEM] * 10,
        [shape_of((rows, 4 * T)), shape_of((32, 24, T))] + [shape_of((rows, 2 * width))] * 2 + [shape_of((rows, width))],
        [
            pltpu.VMEM((6, rows, T), BF),
            pltpu.VMEM((6, rows, T), BF),
            pltpu.VMEM((6 * T, 4 * T), BF),
            pltpu.VMEM((6 * T, 4 * T), BF),
            pltpu.VMEM((rows, 4 * T), BF),
            pltpu.VMEM((rows, 4 * T), BF),
            pltpu.VMEM((rows, 4 * T), BF),
            pltpu.VMEM((rows, 4 * T), BF),
            pltpu.VMEM((5 * rows, 2 * T), F32),
        ],
        15 * 10**8,
        10**7,
        "layer",
        20,
    )(
        where, tile_offsets, mixed, got, swapped, mine, weight_got, weight_swapped,
        bias.reshape(1, -1), grad_out, rdeg, t_hl,
    )
    with jax.named_scope("nodes_sum"):
        held = jnp.sum(lax.all_to_all(parts, PLANE, 0, 0), axis=0)
    with jax.named_scope("back_halo"):
        came = by_core(q_far, NODES, 1, -1)
    with jax.named_scope("nodes_sum"):
        held = jnp.broadcast_to(held[None], (4, 24, T))
        held = jnp.sum(lax.all_to_all(held, "zh", 0, 0), axis=0)
    with jax.named_scope("back_halo"):
        came, held = lax.optimization_barrier((q_near + came, held))
        came = by_core(came, NODES, 1, -1)
        lent = swap(jnp.where(c == 0, came[:, width:], came[:, :width]))
        grad_features = center + (jnp.where(c == 0, came[:, :width], came[:, width:]) + lent)
    with jax.named_scope("nodes_sum"):
        grad_bias = held[16:20].reshape(-1)
        whole = jnp.broadcast_to(held[None, :16], (32, 16, T))
        whole = lax.all_to_all(whole, PLANE, 0, 0)
    (grad_weight,) = call(
        arrange_kernel, [VMEM], [shape_of((T, 4 * T))], [], 10**3, 5 * 10**5, "arrange", 4
    )(whole)
    return output, grad_features, grad_weight, grad_bias


def solution(mesh):
    fine = Mesh(mesh.devices.reshape(4, 8, 4, 3, 2), NODES + YEARS)
    placed = (
        P(NODES, YEARS),
        P(YEARS, None),
        P(),
        P(NODES, None, None, None),
        P(NODES, None),
        P(NODES),
        P(NODES, None),
    )
    return jax.shard_map(
        body,
        mesh=fine,
        in_specs=placed,
        out_specs=(P(NODES, None), P(NODES, YEARS), P(YEARS, None), P()),
        check_vma=False,
    )
```

```python
import jax
import jax.numpy as jnp
from jax import lax
from jax.experimental import pallas as pl
from jax.experimental.pallas import tpu as pltpu
from jax.sharding import Mesh, PartitionSpec as P

NODES = ("x", "y", "zh")
YEARS = ("zl", "c")
PLANE = ("x", "y")
REACH = 2
T = 128
F32 = jnp.float32
BF = jnp.bfloat16
VMEM = pl.BlockSpec(memory_space=pltpu.VMEM)
SMEM = pl.BlockSpec(memory_space=pltpu.SMEM)


def shape_of(shape, dtype=F32):
    return jax.ShapeDtypeStruct(shape, dtype)


def call(kernel, ins, outs, scratch, flops, bytes_accessed, name, limit):
    return pl.pallas_call(
        kernel,
        in_specs=ins,
        out_specs=[VMEM] * len(outs),
        out_shape=outs,
        scratch_shapes=scratch,
        name=name,
        cost_estimate=pl.CostEstimate(
            flops=flops, bytes_accessed=bytes_accessed, transcendentals=0
        ),
        compiler_params=pltpu.CompilerParams(vmem_limit_bytes=limit * 2**20),
    )


def split(v):
    hi = v.astype(BF)
    lo = (v - hi.astype(F32)).astype(BF)
    return hi, lo


def dot(a, b):
    return lax.dot_general(a, b, (((1,), (0,)), ((), ())), preferred_element_type=F32)


def dot_t(a, b):
    return lax.dot_general(a, b, (((1,), (1,)), ((), ())), preferred_element_type=F32)


def prepare_kernel(count, tiles, a_hi, a_lo, t_hl, rdeg):
    for t in range(tiles.shape[0]):
        total = jnp.zeros((T, T), F32)
        for s in range(tiles.shape[1]):
            live = jnp.where(s < count[t], 1.0, 0.0).astype(F32)
            a = tiles[t, s] * live
            total = total + a
            cols = slice(s * T, (s + 1) * T)
            hi, lo = split(a)
            a_hi[t, :, cols] = hi
            a_lo[t, :, cols] = lo
            hi, lo = split(a.T)
            t_hl[t, cols, :T] = hi
            t_hl[t, cols, T:] = lo
        degree = 1.0 + jnp.sum(total, axis=1, keepdims=True)
        rdeg[t * T : (t + 1) * T, :] = jnp.broadcast_to(1.0 / degree, (T, T))


def window_index(offset, t, s):
    return jnp.clip(t + offset[t, s] + 2 * 4, 0, 19)


def mix_kernel(
    where, offset, far, far2, near, near2, own, other, a_hi, a_lo, partial, sent, window
):
    rows = own.shape[0]
    c = where[0]
    for refs, shard in (((far, far2), 4 * c), ((near, near2), 1 + 2 * c), ((own, other), 2)):
        at = pl.multiple_of(shard * rows, rows)
        for k in range(2):
            hi, lo = split(refs[k][...])
            window[pl.ds(at, rows), k * T : (k + 1) * T] = hi
            window[pl.ds(at, rows), (2 + k) * T : (3 + k) * T] = lo
    window[5 * rows :, :] = jnp.zeros((T, 4 * T), BF)
    low, high = 12 * c, 12 + 8 * c
    first = (1 - c).astype(F32)
    for t in range(a_hi.shape[0]):
        picked = []
        for s in range(4):
            w = window_index(offset, t, s)
            w = jnp.where((w >= low) & (w < high), w, 20)
            picked.append(window[pl.ds(pl.multiple_of(w * T, T), T), :])
        b = jnp.concatenate(picked, axis=0)
        wide = dot(a_hi[t], b)
        total = wide[:, : 2 * T] + wide[:, 2 * T :] + dot(a_lo[t], b[:, : 2 * T])
        r = slice(t * T, (t + 1) * T)
        for k in range(2):
            value = total[:, k * T : (k + 1) * T] + (own, other)[k][r, :] * first
            partial[k, r, :] = value
            sent[1 - k, r, :] = value


def layer_kernel(
    where, offset, mixed, got, swapped, weight, weight_got, weight_swapped, bias, gout, rdeg, t_hl,
    output, parts, far, near, center, m_hi, m_lo, w_hi, w_lo, s_hi, s_lo, g_hi, g_lo, back,
):
    rows = gout.shape[0]
    c, zl = where[0], where[1]
    arrived = (
        (mixed, weight, 0, c),
        (got, weight_got, 1 + c, c),
        (swapped, weight_swapped, 2 - c, 1 - c),
    )
    for ref, ref_w, back_by, core in arrived:
        chip = lax.rem(zl - back_by + 3, 3)
        for k in range(2):
            block = chip * 2 + (core if k == 0 else 1 - core)
            hi, lo = split(ref[k])
            m_hi[block] = hi
            m_lo[block] = lo
            hi, lo = split(ref_w[k])
            at = pl.ds(pl.multiple_of(block * T, T), T)
            w_hi[at, :] = hi
            w_lo[at, :] = lo
    back[...] = jnp.zeros_like(back)
    line = jnp.zeros((1, 4 * T), F32)
    for t in range(rows // T):
        r = slice(t * T, (t + 1) * T)
        mh = jnp.concatenate([m_hi[k, r, :] for k in range(6)], axis=1)
        ml = jnp.concatenate([m_lo[k, r, :] for k in range(6)], axis=1)
        pre = dot(mh, w_hi[...]) + dot(mh, w_lo[...]) + dot(ml, w_hi[...]) + bias[...]
        sigma = 1.0 / (1.0 + jnp.exp(-pre))
        output[r, :] = pre * sigma
        g = gout[r, :] * sigma * (1.0 + pre * (1.0 - sigma))
        line = line + jnp.sum(g, axis=0, keepdims=True)
        hi, lo = split(g)
        g_hi[r, :] = hi
        g_lo[r, :] = lo
        scale = rdeg[r, :]
        hi, lo = split(g * jnp.concatenate([scale] * 4, axis=1))
        s_hi[r, :] = hi
        s_lo[r, :] = lo
    mine = pl.ds(pl.multiple_of(zl * (2 * T), 2 * T), 2 * T)
    wh, wl = w_hi[mine, :], w_lo[mine, :]
    z = dot_t(s_hi[...], wh) + dot_t(s_hi[...], wl) + dot_t(s_lo[...], wh)
    back[REACH * rows : (REACH + 1) * rows, :] = z
    zh, zo = split(z)
    for t in range(rows // T):
        r = slice(t * T, (t + 1) * T)
        both = jnp.concatenate([zh[r, :], zh[r, :]], axis=0)
        contrib = dot(t_hl[t], both) + dot(t_hl[t, :, :T], zo[r, :])
        for s in range(4):
            at = pl.multiple_of(window_index(offset, t, s) * T, T)
            back[pl.ds(at, T), :] += contrib[s * T : (s + 1) * T, :]
    far[...] = back[pl.ds(pl.multiple_of((4 - 4 * c) * rows, rows), rows), :]
    near[...] = back[pl.ds(pl.multiple_of((3 - 2 * c) * rows, rows), rows), :]
    mid = back[REACH * rows : (REACH + 1) * rows, :]
    center[...] = jnp.where(c == 0, mid[:, :T], mid[:, T:])
    own = mixed[0]
    m = jnp.concatenate([own[t * T : (t + 1) * T, :].T for t in range(rows // T)], axis=1)
    mh, ml = split(m)
    total = dot(mh, g_hi[...]) + dot(mh, g_lo[...]) + dot(ml, g_hi[...])
    for p in range(32):
        cols = slice((p % 4) * T, (p % 4 + 1) * T)
        parts[p, 0:16, :] = total[(p // 4) * 16 : (p // 4 + 1) * 16, cols]
        for k in range(4):
            parts[p, 16 + k : 17 + k, :] = line[:, k * T : (k + 1) * T]
        parts[p, 20:24, :] = jnp.zeros((4, T), F32)


def arrange_kernel(pieces, out):
    for p in range(32):
        out[(p // 4) * 16 : (p // 4 + 1) * 16, (p % 4) * T : (p % 4 + 1) * T] = pieces[p]


def by_core(block, axis, first, second):
    n = lax.axis_size(axis)
    route = [(2 * i + c, 2 * ((i + d) % n) + c) for i in range(n) for c, d in ((0, first), (1, second))]
    axes = (axis if isinstance(axis, tuple) else (axis,)) + ("c",)
    return lax.ppermute(block, axes, route)


def swap(block):
    return lax.ppermute(block, "c", [(0, 1), (1, 0)])


def body(features, weight, bias, tile_weights, tile_offsets, tile_counts, grad_out):
    rows, width = features.shape
    tiles = tile_weights.shape[0]
    zl, c = lax.axis_index("zl"), lax.axis_index("c")
    where = jnp.stack([c, zl]).astype(jnp.int32)

    with jax.named_scope("halo"):
        other = swap(features)
        near = by_core(features, NODES, 1, -1)
        near2 = by_core(other, NODES, 1, -1)
        far = by_core(near, NODES, 1, -1)
        far2 = by_core(near2, NODES, 1, -1)
    with jax.named_scope("weight_gather"):
        other_weight = swap(weight)
        mine = jnp.stack([weight, other_weight])
        odd = lax.axis_index("x") % 2
        half = lax.dynamic_slice(mine, (0, odd * (T // 2), 0), (2, T // 2, 4 * T))
        half, near2 = lax.optimization_barrier((half, near2))
        half = by_core(half, "zl", 1, 2)
        theirs = lax.ppermute(half, "x", [(i, i ^ 1) for i in range(4)])
        weight_got = jnp.where(
            odd == 0, jnp.concatenate([half, theirs], 1), jnp.concatenate([theirs, half], 1)
        )
        weight_swapped = swap(weight_got)

    a_hi, a_lo, t_hl, rdeg = call(
        prepare_kernel,
        [SMEM, VMEM],
        [
            shape_of((tiles, T, 4 * T), BF),
            shape_of((tiles, T, 4 * T), BF),
            shape_of((tiles, 4 * T, 2 * T), BF),
            shape_of((rows, T)),
        ],
        [],
        10**6,
        4 * 10**6,
        "prepare",
        8,
    )(tile_counts, tile_weights)
    partial, sent = call(
        mix_kernel,
        [SMEM] * 2 + [VMEM] * 8,
        [shape_of((2, rows, width))] * 2,
        [pltpu.VMEM((5 * rows + T, 4 * T), BF)],
        2 * 10**8,
        3 * 10**6,
        "mix",
        12,
    )(where, tile_offsets, far, far2, near, near2, features, other, a_hi, a_lo)
    with jax.named_scope("mixed_gather"):
        mixed = (partial + swap(sent)) * rdeg[None]
        got = by_core(mixed, "zl", 1, 2)
        swapped = swap(got)
    output, parts, q_far, q_near, center = call(
        layer_kernel,
        [SMEM] * 2 + [VMEM] * 10,
        [shape_of((rows, 4 * T)), shape_of((32, 24, T))] + [shape_of((rows, 2 * width))] * 2 + [shape_of((rows, width))],
        [
            pltpu.VMEM((6, rows, T), BF),
            pltpu.VMEM((6, rows, T), BF),
            pltpu.VMEM((6 * T, 4 * T), BF),
            pltpu.VMEM((6 * T, 4 * T), BF),
            pltpu.VMEM((rows, 4 * T), BF),
            pltpu.VMEM((rows, 4 * T), BF),
            pltpu.VMEM((rows, 4 * T), BF),
            pltpu.VMEM((rows, 4 * T), BF),
            pltpu.VMEM((5 * rows, 2 * T), F32),
        ],
        15 * 10**8,
        10**7,
        "layer",
        20,
    )(
        where, tile_offsets, mixed, got, swapped, mine, weight_got, weight_swapped,
        bias.reshape(1, -1), grad_out, rdeg, t_hl,
    )
    with jax.named_scope("nodes_sum"):
        held = jnp.sum(lax.all_to_all(parts, PLANE, 0, 0), axis=0)
    with jax.named_scope("back_halo"):
        came = by_core(q_far, NODES, 1, -1)
    with jax.named_scope("nodes_sum"):
        held = jnp.broadcast_to(held[None], (4, 24, T))
        held = jnp.sum(lax.all_to_all(held, "zh", 0, 0), axis=0)
    with jax.named_scope("back_halo"):
        came, held = lax.optimization_barrier((q_near + came, held))
        came = by_core(came, NODES, 1, -1)
        lent = swap(jnp.where(c == 0, came[:, width:], came[:, :width]))
        grad_features = center + (jnp.where(c == 0, came[:, :width], came[:, width:]) + lent)
    with jax.named_scope("nodes_sum"):
        grad_bias = held[16:20].reshape(-1)
        whole = jnp.broadcast_to(held[None, :16], (32, 16, T))
        whole = lax.all_to_all(whole, PLANE, 0, 0)
    (grad_weight,) = call(
        arrange_kernel, [VMEM], [shape_of((T, 4 * T))], [], 10**3, 5 * 10**5, "arrange", 4
    )(whole)
    return output, grad_features, grad_weight, grad_bias


def solution(mesh):
    fine = Mesh(mesh.devices.reshape(4, 8, 4, 3, 2), NODES + YEARS)
    placed = (
        P(NODES, YEARS),
        P(YEARS, None),
        P(),
        P(NODES, None, None, None),
        P(NODES, None),
        P(NODES),
        P(NODES, None),
    )
    return jax.shard_map(
        body,
        mesh=fine,
        in_specs=placed,
        out_specs=(P(NODES, None), P(NODES, YEARS), P(YEARS, None), P()),
        check_vma=False,
    )
```

```python
import jax
import jax.numpy as jnp
from jax import lax
from jax.experimental import pallas as pl
from jax.experimental.pallas import tpu as pltpu
from jax.sharding import Mesh, PartitionSpec as P

NODES = ("x", "y", "zh")
YEARS = ("zl", "c")
PLANE = ("x", "y")
REACH = 2
T = 128
F32 = jnp.float32
BF = jnp.bfloat16
VMEM = pl.BlockSpec(memory_space=pltpu.VMEM)
SMEM = pl.BlockSpec(memory_space=pltpu.SMEM)


def shape_of(shape, dtype=F32):
    return jax.ShapeDtypeStruct(shape, dtype)


def call(kernel, ins, outs, scratch, flops, bytes_accessed, name, limit):
    return pl.pallas_call(
        kernel,
        in_specs=ins,
        out_specs=[VMEM] * len(outs),
        out_shape=outs,
        scratch_shapes=scratch,
        name=name,
        cost_estimate=pl.CostEstimate(
            flops=flops, bytes_accessed=bytes_accessed, transcendentals=0
        ),
        compiler_params=pltpu.CompilerParams(vmem_limit_bytes=limit * 2**20),
    )


def split(v):
    hi = v.astype(BF)
    lo = (v - hi.astype(F32)).astype(BF)
    return hi, lo


def dot(a, b):
    return lax.dot_general(a, b, (((1,), (0,)), ((), ())), preferred_element_type=F32)


def dot_t(a, b):
    return lax.dot_general(a, b, (((1,), (1,)), ((), ())), preferred_element_type=F32)


def prepare_kernel(count, tiles, a_hi, a_lo, t_hl, rdeg):
    for t in range(tiles.shape[0]):
        total = jnp.zeros((T, T), F32)
        for s in range(tiles.shape[1]):
            live = jnp.where(s < count[t], 1.0, 0.0).astype(F32)
            a = tiles[t, s] * live
            total = total + a
            cols = slice(s * T, (s + 1) * T)
            hi, lo = split(a)
            a_hi[t, :, cols] = hi
            a_lo[t, :, cols] = lo
            hi, lo = split(a.T)
            t_hl[t, cols, :T] = hi
            t_hl[t, cols, T:] = lo
        degree = 1.0 + jnp.sum(total, axis=1, keepdims=True)
        rdeg[t * T : (t + 1) * T, :] = jnp.broadcast_to(1.0 / degree, (T, T))


def window_index(offset, t, s):
    return jnp.clip(t + offset[t, s] + 2 * 4, 0, 19)


def mix_kernel(
    where, offset, far, far2, near, near2, own, other, a_hi, a_lo, partial, sent, window
):
    rows = own.shape[0]
    c = where[0]
    for refs, shard in (((far, far2), 4 * c), ((near, near2), 1 + 2 * c), ((own, other), 2)):
        at = pl.multiple_of(shard * rows, rows)
        for k in range(2):
            hi, lo = split(refs[k][...])
            window[pl.ds(at, rows), k * T : (k + 1) * T] = hi
            window[pl.ds(at, rows), (2 + k) * T : (3 + k) * T] = lo
    window[5 * rows :, :] = jnp.zeros((T, 4 * T), BF)
    low, high = 12 * c, 12 + 8 * c
    first = (1 - c).astype(F32)
    for t in range(a_hi.shape[0]):
        picked = []
        for s in range(4):
            w = window_index(offset, t, s)
            w = jnp.where((w >= low) & (w < high), w, 20)
            picked.append(window[pl.ds(pl.multiple_of(w * T, T), T), :])
        b = jnp.concatenate(picked, axis=0)
        wide = dot(a_hi[t], b)
        total = wide[:, : 2 * T] + wide[:, 2 * T :] + dot(a_lo[t], b[:, : 2 * T])
        r = slice(t * T, (t + 1) * T)
        for k in range(2):
            value = total[:, k * T : (k + 1) * T] + (own, other)[k][r, :] * first
            partial[k, r, :] = value
            sent[1 - k, r, :] = value


def layer_kernel(
    where, offset, mixed, got, swapped, weight, weight_got, weight_swapped, bias, gout, rdeg, t_hl,
    output, parts, far, near, beyond, center, m_hi, m_lo, w_hi, w_lo, s_hi, s_lo, g_hi, g_lo, back,
):
    rows = gout.shape[0]
    c, zl = where[0], where[1]
    arrived = (
        (mixed, weight, 0, c),
        (got, weight_got, 1 + c, c),
        (swapped, weight_swapped, 2 - c, 1 - c),
    )
    for ref, ref_w, back_by, core in arrived:
        chip = lax.rem(zl - back_by + 3, 3)
        for k in range(2):
            block = chip * 2 + (core if k == 0 else 1 - core)
            hi, lo = split(ref[k])
            m_hi[block] = hi
            m_lo[block] = lo
            hi, lo = split(ref_w[k])
            at = pl.ds(pl.multiple_of(block * T, T), T)
            w_hi[at, :] = hi
            w_lo[at, :] = lo
    back[...] = jnp.zeros_like(back)
    line = jnp.zeros((1, 4 * T), F32)
    for t in range(rows // T):
        r = slice(t * T, (t + 1) * T)
        mh = jnp.concatenate([m_hi[k, r, :] for k in range(6)], axis=1)
        ml = jnp.concatenate([m_lo[k, r, :] for k in range(6)], axis=1)
        pre = dot(mh, w_hi[...]) + dot(mh, w_lo[...]) + dot(ml, w_hi[...]) + bias[...]
        sigma = 1.0 / (1.0 + jnp.exp(-pre))
        output[r, :] = pre * sigma
        g = gout[r, :] * sigma * (1.0 + pre * (1.0 - sigma))
        line = line + jnp.sum(g, axis=0, keepdims=True)
        hi, lo = split(g)
        g_hi[r, :] = hi
        g_lo[r, :] = lo
        scale = rdeg[r, :]
        hi, lo = split(g * jnp.concatenate([scale] * 4, axis=1))
        s_hi[r, :] = hi
        s_lo[r, :] = lo
    mine = pl.ds(pl.multiple_of(zl * (2 * T), 2 * T), 2 * T)
    wh, wl = w_hi[mine, :], w_lo[mine, :]
    z = dot_t(s_hi[...], wh) + dot_t(s_hi[...], wl) + dot_t(s_lo[...], wh)
    back[REACH * rows : (REACH + 1) * rows, :] = z
    zh, zo = split(z)
    for t in range(rows // T):
        r = slice(t * T, (t + 1) * T)
        both = jnp.concatenate([zh[r, :], zh[r, :]], axis=0)
        contrib = dot(t_hl[t], both) + dot(t_hl[t, :, :T], zo[r, :])
        for s in range(4):
            at = pl.multiple_of(window_index(offset, t, s) * T, T)
            back[pl.ds(at, T), :] += contrib[s * T : (s + 1) * T, :]
    far[...] = back[pl.ds(pl.multiple_of((4 - 4 * c) * rows, rows), rows), :]
    side = back[pl.ds(pl.multiple_of((3 - 2 * c) * rows, rows), rows), :]
    near[...] = jnp.where(c == 0, side[:, :T], side[:, T:])
    beyond[...] = jnp.where(c == 0, side[:, T:], side[:, :T])
    mid = back[REACH * rows : (REACH + 1) * rows, :]
    center[...] = jnp.where(c == 0, mid[:, :T], mid[:, T:])
    own = mixed[0]
    m = jnp.concatenate([own[t * T : (t + 1) * T, :].T for t in range(rows // T)], axis=1)
    mh, ml = split(m)
    total = dot(mh, g_hi[...]) + dot(mh, g_lo[...]) + dot(ml, g_hi[...])
    for p in range(32):
        cols = slice((p % 4) * T, (p % 4 + 1) * T)
        parts[p, 0:16, :] = total[(p // 4) * 16 : (p // 4 + 1) * 16, cols]
        for k in range(4):
            parts[p, 16 + k : 17 + k, :] = line[:, k * T : (k + 1) * T]
        parts[p, 20:24, :] = jnp.zeros((4, T), F32)


def arrange_kernel(pieces, out):
    for p in range(32):
        out[(p // 4) * 16 : (p // 4 + 1) * 16, (p % 4) * T : (p % 4 + 1) * T] = pieces[p]


def by_core(block, axis, first, second, cross=False):
    n = lax.axis_size(axis)
    route = [
        (2 * i + c, 2 * ((i + d) % n) + (1 - c if cross else c))
        for i in range(n)
        for c, d in ((0, first), (1, second))
    ]
    axes = (axis if isinstance(axis, tuple) else (axis,)) + ("c",)
    return lax.ppermute(block, axes, route)


def swap(block):
    return lax.ppermute(block, "c", [(0, 1), (1, 0)])


def body(features, weight, bias, tile_weights, tile_offsets, tile_counts, grad_out):
    rows, width = features.shape
    tiles = tile_weights.shape[0]
    zl, c = lax.axis_index("zl"), lax.axis_index("c")
    where = jnp.stack([c, zl]).astype(jnp.int32)

    with jax.named_scope("halo"):
        other = swap(features)
        near = by_core(features, NODES, 1, -1)
        near2 = by_core(other, NODES, 1, -1)
        far = by_core(near, NODES, 1, -1)
        far2 = by_core(near2, NODES, 1, -1)
    with jax.named_scope("weight_gather"):
        other_weight = swap(weight)
        mine = jnp.stack([weight, other_weight])
        odd = lax.axis_index("x") % 2
        half = lax.dynamic_slice(mine, (0, odd * (T // 2), 0), (2, T // 2, 4 * T))
        half, near2 = lax.optimization_barrier((half, near2))
        half = by_core(half, "zl", 1, 2)
        theirs = lax.ppermute(half, "x", [(i, i ^ 1) for i in range(4)])
        weight_got = jnp.where(
            odd == 0, jnp.concatenate([half, theirs], 1), jnp.concatenate([theirs, half], 1)
        )
        weight_swapped = swap(weight_got)

    a_hi, a_lo, t_hl, rdeg = call(
        prepare_kernel,
        [SMEM, VMEM],
        [
            shape_of((tiles, T, 4 * T), BF),
            shape_of((tiles, T, 4 * T), BF),
            shape_of((tiles, 4 * T, 2 * T), BF),
            shape_of((rows, T)),
        ],
        [],
        10**6,
        4 * 10**6,
        "prepare",
        8,
    )(tile_counts, tile_weights)
    partial, sent = call(
        mix_kernel,
        [SMEM] * 2 + [VMEM] * 8,
        [shape_of((2, rows, width))] * 2,
        [pltpu.VMEM((5 * rows + T, 4 * T), BF)],
        2 * 10**8,
        3 * 10**6,
        "mix",
        12,
    )(where, tile_offsets, far, far2, near, near2, features, other, a_hi, a_lo)
    with jax.named_scope("mixed_gather"):
        mixed = (partial + swap(sent)) * rdeg[None]
        got = by_core(mixed, "zl", 1, 2)
        swapped = swap(got)
    output, parts, q_far, q_near, q_other, center = call(
        layer_kernel,
        [SMEM] * 2 + [VMEM] * 10,
        [shape_of((rows, 4 * T)), shape_of((32, 24, T))] + [shape_of((rows, 2 * width))] + [shape_of((rows, width))] * 3,
        [
            pltpu.VMEM((6, rows, T), BF),
            pltpu.VMEM((6, rows, T), BF),
            pltpu.VMEM((6 * T, 4 * T), BF),
            pltpu.VMEM((6 * T, 4 * T), BF),
            pltpu.VMEM((rows, 4 * T), BF),
            pltpu.VMEM((rows, 4 * T), BF),
            pltpu.VMEM((rows, 4 * T), BF),
            pltpu.VMEM((rows, 4 * T), BF),
            pltpu.VMEM((5 * rows, 2 * T), F32),
        ],
        15 * 10**8,
        10**7,
        "layer",
        20,
    )(
        where, tile_offsets, mixed, got, swapped, mine, weight_got, weight_swapped,
        bias.reshape(1, -1), grad_out, rdeg, t_hl,
    )
    with jax.named_scope("nodes_sum"):
        held = jnp.sum(lax.all_to_all(parts, PLANE, 0, 0), axis=0)
    with jax.named_scope("back_halo"):
        came = by_core(q_far, NODES, 1, -1)
    with jax.named_scope("nodes_sum"):
        held = jnp.broadcast_to(held[None], (4, 24, T))
        held = jnp.sum(lax.all_to_all(held, "zh", 0, 0), axis=0)
    with jax.named_scope("back_halo"):
        came, held = lax.optimization_barrier((came, held))
        kept = q_near + jnp.where(c == 0, came[:, :width], came[:, width:])
        lent = q_other + jnp.where(c == 0, came[:, width:], came[:, :width])
        grad_features = center + (by_core(kept, NODES, 1, -1) + by_core(lent, NODES, 1, -1, True))
    with jax.named_scope("nodes_sum"):
        grad_bias = held[16:20].reshape(-1)
        whole = jnp.broadcast_to(held[None, :16], (32, 16, T))
        whole = lax.all_to_all(whole, PLANE, 0, 0)
    (grad_weight,) = call(
        arrange_kernel, [VMEM], [shape_of((T, 4 * T))], [], 10**3, 5 * 10**5, "arrange", 4
    )(whole)
    return output, grad_features, grad_weight, grad_bias


def solution(mesh):
    fine = Mesh(mesh.devices.reshape(4, 8, 4, 3, 2), NODES + YEARS)
    placed = (
        P(NODES, YEARS),
        P(YEARS, None),
        P(),
        P(NODES, None, None, None),
        P(NODES, None),
        P(NODES),
        P(NODES, None),
    )
    return jax.shard_map(
        body,
        mesh=fine,
        in_specs=placed,
        out_specs=(P(NODES, None), P(NODES, YEARS), P(YEARS, None), P()),
        check_vma=False,
    )
```

```python
import jax
import jax.numpy as jnp
from jax import lax
from jax.experimental import pallas as pl
from jax.experimental.pallas import tpu as pltpu
from jax.sharding import Mesh, PartitionSpec as P

NODES = ("x", "y", "zh")
YEARS = ("zl", "c")
PLANE = ("x", "y")
REACH = 2
T = 128
F32 = jnp.float32
BF = jnp.bfloat16
VMEM = pl.BlockSpec(memory_space=pltpu.VMEM)
SMEM = pl.BlockSpec(memory_space=pltpu.SMEM)


def shape_of(shape, dtype=F32):
    return jax.ShapeDtypeStruct(shape, dtype)


def call(kernel, ins, outs, scratch, flops, bytes_accessed, name, limit):
    return pl.pallas_call(
        kernel,
        in_specs=ins,
        out_specs=[VMEM] * len(outs),
        out_shape=outs,
        scratch_shapes=scratch,
        name=name,
        cost_estimate=pl.CostEstimate(
            flops=flops, bytes_accessed=bytes_accessed, transcendentals=0
        ),
        compiler_params=pltpu.CompilerParams(vmem_limit_bytes=limit * 2**20),
    )


def split(v):
    hi = v.astype(BF)
    lo = (v - hi.astype(F32)).astype(BF)
    return hi, lo


def dot(a, b):
    return lax.dot_general(a, b, (((1,), (0,)), ((), ())), preferred_element_type=F32)


def dot_t(a, b):
    return lax.dot_general(a, b, (((1,), (1,)), ((), ())), preferred_element_type=F32)


def prepare_kernel(count, tiles, a_hi, a_lo, t_hl, rdeg):
    for t in range(tiles.shape[0]):
        total = jnp.zeros((T, T), F32)
        for s in range(tiles.shape[1]):
            live = jnp.where(s < count[t], 1.0, 0.0).astype(F32)
            a = tiles[t, s] * live
            total = total + a
            cols = slice(s * T, (s + 1) * T)
            hi, lo = split(a)
            a_hi[t, :, cols] = hi
            a_lo[t, :, cols] = lo
            hi, lo = split(a.T)
            t_hl[t, cols, :T] = hi
            t_hl[t, cols, T:] = lo
        degree = 1.0 + jnp.sum(total, axis=1, keepdims=True)
        rdeg[t * T : (t + 1) * T, :] = jnp.broadcast_to(1.0 / degree, (T, T))


def window_index(offset, t, s):
    return jnp.clip(t + offset[t, s] + 2 * 4, 0, 19)


def mix_kernel(
    where, offset, far, far2, near, near2, own, other, a_hi, a_lo, partial, sent, window
):
    rows = own.shape[0]
    c = where[0]
    for refs, shard in (((far, far2), 4 * c), ((near, near2), 1 + 2 * c), ((own, other), 2)):
        at = pl.multiple_of(shard * rows, rows)
        for k in range(2):
            hi, lo = split(refs[k][...])
            window[pl.ds(at, rows), k * T : (k + 1) * T] = hi
            window[pl.ds(at, rows), (2 + k) * T : (3 + k) * T] = lo
    window[5 * rows :, :] = jnp.zeros((T, 4 * T), BF)
    low, high = 12 * c, 12 + 8 * c
    first = (1 - c).astype(F32)
    for t in range(a_hi.shape[0]):
        picked = []
        for s in range(4):
            w = window_index(offset, t, s)
            w = jnp.where((w >= low) & (w < high), w, 20)
            picked.append(window[pl.ds(pl.multiple_of(w * T, T), T), :])
        b = jnp.concatenate(picked, axis=0)
        wide = dot(a_hi[t], b)
        total = wide[:, : 2 * T] + wide[:, 2 * T :] + dot(a_lo[t], b[:, : 2 * T])
        r = slice(t * T, (t + 1) * T)
        for k in range(2):
            value = total[:, k * T : (k + 1) * T] + (own, other)[k][r, :] * first
            partial[k, r, :] = value
            sent[1 - k, r, :] = value


def layer_kernel(
    where, offset, mixed, got, swapped, weight, weight_got, weight_swapped, bias, gout, rdeg, t_hl,
    output, parts, far, near, beyond, center, m_hi, m_lo, w_hi, w_lo, s_hi, s_lo, g_hi, g_lo, back,
):
    rows = gout.shape[0]
    c, zl = where[0], where[1]
    arrived = (
        (mixed, weight, 0, c),
        (got, weight_got, 1 + c, c),
        (swapped, weight_swapped, 2 - c, 1 - c),
    )
    for ref, ref_w, back_by, core in arrived:
        chip = lax.rem(zl - back_by + 3, 3)
        for k in range(2):
            block = chip * 2 + (core if k == 0 else 1 - core)
            hi, lo = split(ref[k])
            m_hi[block] = hi
            m_lo[block] = lo
            hi, lo = split(ref_w[k])
            at = pl.ds(pl.multiple_of(block * T, T), T)
            w_hi[at, :] = hi
            w_lo[at, :] = lo
    back[...] = jnp.zeros_like(back)
    line = jnp.zeros((1, 4 * T), F32)
    for t in range(rows // T):
        r = slice(t * T, (t + 1) * T)
        mh = jnp.concatenate([m_hi[k, r, :] for k in range(6)], axis=1)
        ml = jnp.concatenate([m_lo[k, r, :] for k in range(6)], axis=1)
        pre = dot(mh, w_hi[...]) + dot(mh, w_lo[...]) + dot(ml, w_hi[...]) + bias[...]
        sigma = 1.0 / (1.0 + jnp.exp(-pre))
        output[r, :] = pre * sigma
        g = gout[r, :] * sigma * (1.0 + pre * (1.0 - sigma))
        line = line + jnp.sum(g, axis=0, keepdims=True)
        hi, lo = split(g)
        g_hi[r, :] = hi
        g_lo[r, :] = lo
        scale = rdeg[r, :]
        hi, lo = split(g * jnp.concatenate([scale] * 4, axis=1))
        s_hi[r, :] = hi
        s_lo[r, :] = lo
    mine = pl.ds(pl.multiple_of(zl * (2 * T), 2 * T), 2 * T)
    wh, wl = w_hi[mine, :], w_lo[mine, :]
    z = dot_t(s_hi[...], wh) + dot_t(s_hi[...], wl) + dot_t(s_lo[...], wh)
    back[REACH * rows : (REACH + 1) * rows, :] = z
    zh, zo = split(z)
    for t in range(rows // T):
        r = slice(t * T, (t + 1) * T)
        both = jnp.concatenate([zh[r, :], zh[r, :]], axis=0)
        contrib = dot(t_hl[t], both) + dot(t_hl[t, :, :T], zo[r, :])
        for s in range(4):
            at = pl.multiple_of(window_index(offset, t, s) * T, T)
            back[pl.ds(at, T), :] += contrib[s * T : (s + 1) * T, :]
    far[...] = back[pl.ds(pl.multiple_of((4 - 4 * c) * rows, rows), rows), :]
    side = back[pl.ds(pl.multiple_of((3 - 2 * c) * rows, rows), rows), :]
    near[...] = jnp.where(c == 0, side[:, :T], side[:, T:])
    beyond[...] = jnp.where(c == 0, side[:, T:], side[:, :T])
    mid = back[REACH * rows : (REACH + 1) * rows, :]
    center[...] = jnp.where(c == 0, mid[:, :T], mid[:, T:])
    own = mixed[0]
    m = jnp.concatenate([own[t * T : (t + 1) * T, :].T for t in range(rows // T)], axis=1)
    mh, ml = split(m)
    total = dot(mh, g_hi[...]) + dot(mh, g_lo[...]) + dot(ml, g_hi[...])
    for p in range(32):
        cols = slice((p % 4) * T, (p % 4 + 1) * T)
        parts[p, 0:16, :] = total[(p // 4) * 16 : (p // 4 + 1) * 16, cols]
        for k in range(4):
            parts[p, 16 + k : 17 + k, :] = line[:, k * T : (k + 1) * T]
        parts[p, 20:24, :] = jnp.zeros((4, T), F32)


def arrange_kernel(pieces, out):
    for p in range(32):
        out[(p // 4) * 16 : (p // 4 + 1) * 16, (p % 4) * T : (p % 4 + 1) * T] = pieces[p]


def by_core(block, axis, first, second, cross=False):
    n = lax.axis_size(axis)
    route = [
        (2 * i + c, 2 * ((i + d) % n) + (1 - c if cross else c))
        for i in range(n)
        for c, d in ((0, first), (1, second))
    ]
    axes = (axis if isinstance(axis, tuple) else (axis,)) + ("c",)
    return lax.ppermute(block, axes, route)


def swap(block):
    return lax.ppermute(block, "c", [(0, 1), (1, 0)])


def body(features, weight, bias, tile_weights, tile_offsets, tile_counts, grad_out):
    rows, width = features.shape
    tiles = tile_weights.shape[0]
    zl, c = lax.axis_index("zl"), lax.axis_index("c")
    where = jnp.stack([c, zl]).astype(jnp.int32)

    with jax.named_scope("halo"):
        other = swap(features)
        near = by_core(features, NODES, 1, -1)
        near2 = by_core(other, NODES, 1, -1)
        far = by_core(near, NODES, 1, -1)
        far2 = by_core(near2, NODES, 1, -1)
    with jax.named_scope("weight_gather"):
        other_weight = swap(weight)
        mine = jnp.stack([weight, other_weight])
        odd = lax.axis_index("x") % 2
        half = lax.dynamic_slice(mine, (0, odd * (T // 2), 0), (2, T // 2, 4 * T))
        half, near2 = lax.optimization_barrier((half, near2))
        half = by_core(half, "zl", 1, 2)
        theirs = lax.ppermute(half, "x", [(i, i ^ 1) for i in range(4)])
        weight_got = jnp.where(
            odd == 0, jnp.concatenate([half, theirs], 1), jnp.concatenate([theirs, half], 1)
        )
        weight_swapped = swap(weight_got)

    a_hi, a_lo, t_hl, rdeg = call(
        prepare_kernel,
        [SMEM, VMEM],
        [
            shape_of((tiles, T, 4 * T), BF),
            shape_of((tiles, T, 4 * T), BF),
            shape_of((tiles, 4 * T, 2 * T), BF),
            shape_of((rows, T)),
        ],
        [],
        10**6,
        4 * 10**6,
        "prepare",
        8,
    )(tile_counts, tile_weights)
    partial, sent = call(
        mix_kernel,
        [SMEM] * 2 + [VMEM] * 8,
        [shape_of((2, rows, width))] * 2,
        [pltpu.VMEM((5 * rows + T, 4 * T), BF)],
        2 * 10**8,
        3 * 10**6,
        "mix",
        12,
    )(where, tile_offsets, far, far2, near, near2, features, other, a_hi, a_lo)
    with jax.named_scope("mixed_gather"):
        mixed = (partial + swap(sent)) * rdeg[None]
        got = by_core(mixed, "zl", 1, 2)
        swapped = swap(got)
    output, parts, q_far, q_near, q_other, center = call(
        layer_kernel,
        [SMEM] * 2 + [VMEM] * 10,
        [shape_of((rows, 4 * T)), shape_of((32, 24, T))] + [shape_of((rows, 2 * width))] + [shape_of((rows, width))] * 3,
        [
            pltpu.VMEM((6, rows, T), BF),
            pltpu.VMEM((6, rows, T), BF),
            pltpu.VMEM((6 * T, 4 * T), BF),
            pltpu.VMEM((6 * T, 4 * T), BF),
            pltpu.VMEM((rows, 4 * T), BF),
            pltpu.VMEM((rows, 4 * T), BF),
            pltpu.VMEM((rows, 4 * T), BF),
            pltpu.VMEM((rows, 4 * T), BF),
            pltpu.VMEM((5 * rows, 2 * T), F32),
        ],
        15 * 10**8,
        10**7,
        "layer",
        20,
    )(
        where, tile_offsets, mixed, got, swapped, mine, weight_got, weight_swapped,
        bias.reshape(1, -1), grad_out, rdeg, t_hl,
    )
    with jax.named_scope("nodes_sum"):
        held = jnp.sum(lax.all_to_all(parts, PLANE, 0, 0), axis=0)
    with jax.named_scope("back_halo"):
        came = by_core(q_far, NODES, 1, -1)
    with jax.named_scope("nodes_sum"):
        plane = held
        held = jnp.broadcast_to(held[None], (4, 24, T))
        held = jnp.sum(lax.all_to_all(held, "zh", 0, 0), axis=0)
    with jax.named_scope("back_halo"):
        kept = q_near + plane[:1, :1] * 0.0 + jnp.where(c == 0, came[:, :width], came[:, width:])
        came, held = lax.optimization_barrier((came, held))
        lent = q_other + jnp.where(c == 0, came[:, width:], came[:, :width])
        grad_features = center + (by_core(kept, NODES, 1, -1) + by_core(lent, NODES, 1, -1, True))
    with jax.named_scope("nodes_sum"):
        grad_bias = held[16:20].reshape(-1)
        whole = jnp.broadcast_to(held[None, :16], (32, 16, T))
        whole = lax.all_to_all(whole, PLANE, 0, 0)
    (grad_weight,) = call(
        arrange_kernel, [VMEM], [shape_of((T, 4 * T))], [], 10**3, 5 * 10**5, "arrange", 4
    )(whole)
    return output, grad_features, grad_weight, grad_bias


def solution(mesh):
    fine = Mesh(mesh.devices.reshape(4, 8, 4, 3, 2), NODES + YEARS)
    placed = (
        P(NODES, YEARS),
        P(YEARS, None),
        P(),
        P(NODES, None, None, None),
        P(NODES, None),
        P(NODES),
        P(NODES, None),
    )
    return jax.shard_map(
        body,
        mesh=fine,
        in_specs=placed,
        out_specs=(P(NODES, None), P(NODES, YEARS), P(YEARS, None), P()),
        check_vma=False,
    )
```

```python
import jax
import jax.numpy as jnp
from jax import lax
from jax.experimental import pallas as pl
from jax.experimental.pallas import tpu as pltpu
from jax.sharding import Mesh, PartitionSpec as P

NODES = ("x", "y", "zh")
YEARS = ("zl", "c")
PLANE = ("x", "y")
REACH = 2
T = 128
F32 = jnp.float32
BF = jnp.bfloat16
VMEM = pl.BlockSpec(memory_space=pltpu.VMEM)
SMEM = pl.BlockSpec(memory_space=pltpu.SMEM)


def shape_of(shape, dtype=F32):
    return jax.ShapeDtypeStruct(shape, dtype)


def call(kernel, ins, outs, scratch, flops, bytes_accessed, name, limit):
    return pl.pallas_call(
        kernel,
        in_specs=ins,
        out_specs=[VMEM] * len(outs),
        out_shape=outs,
        scratch_shapes=scratch,
        name=name,
        cost_estimate=pl.CostEstimate(
            flops=flops, bytes_accessed=bytes_accessed, transcendentals=0
        ),
        compiler_params=pltpu.CompilerParams(vmem_limit_bytes=limit * 2**20),
    )


def split(v):
    hi = v.astype(BF)
    lo = (v - hi.astype(F32)).astype(BF)
    return hi, lo


def dot(a, b):
    return lax.dot_general(a, b, (((1,), (0,)), ((), ())), preferred_element_type=F32)


def dot_t(a, b):
    return lax.dot_general(a, b, (((1,), (1,)), ((), ())), preferred_element_type=F32)


def prepare_kernel(count, tiles, a_hi, a_lo, t_hl, rdeg):
    for t in range(tiles.shape[0]):
        total = jnp.zeros((T, T), F32)
        for s in range(tiles.shape[1]):
            live = jnp.where(s < count[t], 1.0, 0.0).astype(F32)
            a = tiles[t, s] * live
            total = total + a
            cols = slice(s * T, (s + 1) * T)
            hi, lo = split(a)
            a_hi[t, :, cols] = hi
            a_lo[t, :, cols] = lo
            hi, lo = split(a.T)
            t_hl[t, cols, :T] = hi
            t_hl[t, cols, T:] = lo
        degree = 1.0 + jnp.sum(total, axis=1, keepdims=True)
        rdeg[t * T : (t + 1) * T, :] = jnp.broadcast_to(1.0 / degree, (T, T))


def window_index(offset, t, s):
    return jnp.clip(t + offset[t, s] + 2 * 4, 0, 19)


def mix_kernel(
    where, offset, far, far2, near, near2, own, other, a_hi, a_lo, partial, sent, window
):
    rows = own.shape[0]
    c = where[0]
    for refs, shard in (((far, far2), 4 * c), ((near, near2), 1 + 2 * c), ((own, other), 2)):
        at = pl.multiple_of(shard * rows, rows)
        for k in range(2):
            hi, lo = split(refs[k][...])
            window[pl.ds(at, rows), k * T : (k + 1) * T] = hi
            window[pl.ds(at, rows), (2 + k) * T : (3 + k) * T] = lo
    window[5 * rows :, :] = jnp.zeros((T, 4 * T), BF)
    low, high = 12 * c, 12 + 8 * c
    first = (1 - c).astype(F32)
    for t in range(a_hi.shape[0]):
        picked = []
        for s in range(4):
            w = window_index(offset, t, s)
            w = jnp.where((w >= low) & (w < high), w, 20)
            picked.append(window[pl.ds(pl.multiple_of(w * T, T), T), :])
        b = jnp.concatenate(picked, axis=0)
        wide = dot(a_hi[t], b)
        total = wide[:, : 2 * T] + wide[:, 2 * T :] + dot(a_lo[t], b[:, : 2 * T])
        r = slice(t * T, (t + 1) * T)
        for k in range(2):
            value = total[:, k * T : (k + 1) * T] + (own, other)[k][r, :] * first
            partial[k, r, :] = value
            sent[1 - k, r, :] = value


def layer_kernel(
    where, offset, mixed, got, swapped, weight, weight_got, weight_swapped, bias, gout, rdeg, t_hl,
    output, parts, far, near, beyond, center, m_hi, m_lo, w_hi, w_lo, s_hi, s_lo, g_hi, g_lo, back,
):
    rows = gout.shape[0]
    c, zl = where[0], where[1]
    arrived = (
        (mixed, weight, 0, c),
        (got, weight_got, 1 + c, c),
        (swapped, weight_swapped, 2 - c, 1 - c),
    )
    for ref, ref_w, back_by, core in arrived:
        chip = lax.rem(zl - back_by + 3, 3)
        for k in range(2):
            block = chip * 2 + (core if k == 0 else 1 - core)
            hi, lo = split(ref[k])
            m_hi[block] = hi
            m_lo[block] = lo
            hi, lo = split(ref_w[k])
            at = pl.ds(pl.multiple_of(block * T, T), T)
            w_hi[at, :] = hi
            w_lo[at, :] = lo
    back[...] = jnp.zeros_like(back)
    line = jnp.zeros((1, 4 * T), F32)
    for t in range(rows // T):
        r = slice(t * T, (t + 1) * T)
        mh = jnp.concatenate([m_hi[k, r, :] for k in range(6)], axis=1)
        ml = jnp.concatenate([m_lo[k, r, :] for k in range(6)], axis=1)
        pre = dot(mh, w_hi[...]) + dot(mh, w_lo[...]) + dot(ml, w_hi[...]) + bias[...]
        sigma = 1.0 / (1.0 + jnp.exp(-pre))
        output[r, :] = pre * sigma
        g = gout[r, :] * sigma * (1.0 + pre * (1.0 - sigma))
        line = line + jnp.sum(g, axis=0, keepdims=True)
        hi, lo = split(g)
        g_hi[r, :] = hi
        g_lo[r, :] = lo
        scale = rdeg[r, :]
        hi, lo = split(g * jnp.concatenate([scale] * 4, axis=1))
        s_hi[r, :] = hi
        s_lo[r, :] = lo
    mine = pl.ds(pl.multiple_of(zl * (2 * T), 2 * T), 2 * T)
    wh, wl = w_hi[mine, :], w_lo[mine, :]
    z = dot_t(s_hi[...], wh) + dot_t(s_hi[...], wl) + dot_t(s_lo[...], wh)
    back[REACH * rows : (REACH + 1) * rows, :] = z
    zh, zo = split(z)
    for t in range(rows // T):
        r = slice(t * T, (t + 1) * T)
        both = jnp.concatenate([zh[r, :], zh[r, :]], axis=0)
        contrib = dot(t_hl[t], both) + dot(t_hl[t, :, :T], zo[r, :])
        for s in range(4):
            at = pl.multiple_of(window_index(offset, t, s) * T, T)
            back[pl.ds(at, T), :] += contrib[s * T : (s + 1) * T, :]
    far[...] = back[pl.ds(pl.multiple_of((4 - 4 * c) * rows, rows), rows), :]
    side = back[pl.ds(pl.multiple_of((3 - 2 * c) * rows, rows), rows), :]
    near[...] = jnp.where(c == 0, side[:, :T], side[:, T:])
    beyond[...] = jnp.where(c == 0, side[:, T:], side[:, :T])
    mid = back[REACH * rows : (REACH + 1) * rows, :]
    center[...] = jnp.where(c == 0, mid[:, :T], mid[:, T:])
    own = mixed[0]
    m = jnp.concatenate([own[t * T : (t + 1) * T, :].T for t in range(rows // T)], axis=1)
    mh, ml = split(m)
    total = dot(mh, g_hi[...]) + dot(mh, g_lo[...]) + dot(ml, g_hi[...])
    for p in range(32):
        cols = slice((p % 4) * T, (p % 4 + 1) * T)
        parts[p, 0:16, :] = total[(p // 4) * 16 : (p // 4 + 1) * 16, cols]
        for k in range(4):
            parts[p, 16 + k : 17 + k, :] = line[:, k * T : (k + 1) * T]
        parts[p, 20:24, :] = jnp.zeros((4, T), F32)


def arrange_kernel(pieces, out):
    for p in range(32):
        out[(p // 4) * 16 : (p // 4 + 1) * 16, (p % 4) * T : (p % 4 + 1) * T] = pieces[p]


def by_core(block, axis, first, second, cross=False):
    n = lax.axis_size(axis)
    route = [
        (2 * i + c, 2 * ((i + d) % n) + (1 - c if cross else c))
        for i in range(n)
        for c, d in ((0, first), (1, second))
    ]
    axes = (axis if isinstance(axis, tuple) else (axis,)) + ("c",)
    return lax.ppermute(block, axes, route)


def swap(block):
    return lax.ppermute(block, "c", [(0, 1), (1, 0)])


def body(features, weight, bias, tile_weights, tile_offsets, tile_counts, grad_out):
    rows, width = features.shape
    tiles = tile_weights.shape[0]
    zl, c = lax.axis_index("zl"), lax.axis_index("c")
    where = jnp.stack([c, zl]).astype(jnp.int32)

    with jax.named_scope("halo"):
        other = swap(features)
        near = by_core(features, NODES, 1, -1)
        near2 = by_core(other, NODES, 1, -1)
        far = by_core(near, NODES, 1, -1)
        far2 = by_core(near2, NODES, 1, -1)
    with jax.named_scope("weight_gather"):
        other_weight = swap(weight)
        mine = jnp.stack([weight, other_weight])
        odd = lax.axis_index("x") % 2
        half = lax.dynamic_slice(mine, (0, odd * (T // 2), 0), (2, T // 2, 4 * T))
        half, near2 = lax.optimization_barrier((half, near2))
        half = by_core(half, "zl", 1, 2)
        theirs = lax.ppermute(half, "x", [(i, i ^ 1) for i in range(4)])
        weight_got = jnp.where(
            odd == 0, jnp.concatenate([half, theirs], 1), jnp.concatenate([theirs, half], 1)
        )
        weight_swapped = swap(weight_got)

    a_hi, a_lo, t_hl, rdeg = call(
        prepare_kernel,
        [SMEM, VMEM],
        [
            shape_of((tiles, T, 4 * T), BF),
            shape_of((tiles, T, 4 * T), BF),
            shape_of((tiles, 4 * T, 2 * T), BF),
            shape_of((rows, T)),
        ],
        [],
        10**6,
        4 * 10**6,
        "prepare",
        8,
    )(tile_counts, tile_weights)
    partial, sent = call(
        mix_kernel,
        [SMEM] * 2 + [VMEM] * 8,
        [shape_of((2, rows, width))] * 2,
        [pltpu.VMEM((5 * rows + T, 4 * T), BF)],
        2 * 10**8,
        3 * 10**6,
        "mix",
        12,
    )(where, tile_offsets, far, far2, near, near2, features, other, a_hi, a_lo)
    with jax.named_scope("mixed_gather"):
        mixed = (partial + swap(sent)) * rdeg[None]
        got = by_core(mixed, "zl", 1, 2)
        swapped = swap(got)
    output, parts, q_far, q_near, q_other, center = call(
        layer_kernel,
        [SMEM] * 2 + [VMEM] * 10,
        [shape_of((rows, 4 * T)), shape_of((32, 24, T))] + [shape_of((rows, 2 * width))] + [shape_of((rows, width))] * 3,
        [
            pltpu.VMEM((6, rows, T), BF),
            pltpu.VMEM((6, rows, T), BF),
            pltpu.VMEM((6 * T, 4 * T), BF),
            pltpu.VMEM((6 * T, 4 * T), BF),
            pltpu.VMEM((rows, 4 * T), BF),
            pltpu.VMEM((rows, 4 * T), BF),
            pltpu.VMEM((rows, 4 * T), BF),
            pltpu.VMEM((rows, 4 * T), BF),
            pltpu.VMEM((5 * rows, 2 * T), F32),
        ],
        15 * 10**8,
        10**7,
        "layer",
        20,
    )(
        where, tile_offsets, mixed, got, swapped, mine, weight_got, weight_swapped,
        bias.reshape(1, -1), grad_out, rdeg, t_hl,
    )
    with jax.named_scope("nodes_sum"):
        held = jnp.sum(lax.all_to_all(parts, PLANE, 0, 0), axis=0)
    with jax.named_scope("back_halo"):
        came = by_core(q_far, NODES, 1, -1)
    with jax.named_scope("nodes_sum"):
        plane = held
        held = jnp.broadcast_to(held[None], (4, 24, T))
        held = jnp.sum(lax.all_to_all(held, "zh", 0, 0), axis=0)
    with jax.named_scope("back_halo"):
        after = plane[:1, :1] * 0.0
        kept = q_near + after + jnp.where(c == 0, came[:, :width], came[:, width:])
        lent = q_other + after + jnp.where(c == 0, came[:, width:], came[:, :width])
        grad_features = center + (by_core(kept, NODES, 1, -1) + by_core(lent, NODES, 1, -1, True))
    with jax.named_scope("nodes_sum"):
        grad_bias = held[16:20].reshape(-1)
        whole = jnp.broadcast_to(held[None, :16], (32, 16, T))
        whole = lax.all_to_all(whole, PLANE, 0, 0)
    (grad_weight,) = call(
        arrange_kernel, [VMEM], [shape_of((T, 4 * T))], [], 10**3, 5 * 10**5, "arrange", 4
    )(whole)
    return output, grad_features, grad_weight, grad_bias


def solution(mesh):
    fine = Mesh(mesh.devices.reshape(4, 8, 4, 3, 2), NODES + YEARS)
    placed = (
        P(NODES, YEARS),
        P(YEARS, None),
        P(),
        P(NODES, None, None, None),
        P(NODES, None),
        P(NODES),
        P(NODES, None),
    )
    return jax.shard_map(
        body,
        mesh=fine,
        in_specs=placed,
        out_specs=(P(NODES, None), P(NODES, YEARS), P(YEARS, None), P()),
        check_vma=False,
    )
```
